32 devices in a mesh: gx: 4 (over y, x), gy: 8 (over z, core).
Axes of the slice: x: 2, y: 2, z: 4, core: 2. Of those that a mesh axis runs over, the one named last changes fastest.
Arguments:
- potential: float32 [96, 128, 128], P('gx', 'gy'), may hold values from -0.875 to 0.875
- density: float32 [96, 128, 128], P('gx', 'gy'), may hold values from 0.5 to 2
- correction: float32 [96, 128, 128], P('gx', 'gy'), may hold values from -6 to 6
Outputs:
- updated: float32 [96, 128, 128], P('gx', 'gy')
- residual: float32 [96, 128, 128], P('gx', 'gy')
The draws below stay inside these ranges and needn't reach their ends.
All inputs are finite; a program needn't handle non-finite values.
Results may differ from the reference program's by a relative error of at most 0.0003.
Values sent between devices are 32-bit elements; how exact they have to be, the bound alone decides.
A program may use at most 64 MiB of HBM per device.

```python
import jax
import jax.numpy as jnp

NZ = 128
FACTOR = 4
PRE = 2
POST = 2
COARSE_SWEEPS = 4
NX = 96
NY = 128


def draw_density(key, part):
    base = jax.random.uniform(key, (NX, NY, NZ), jnp.float32, 0.5, 2.0)
    return base


def block_levels(key, shape, shards, low, largest):
    level = 1.0
    for axis_at, shards_of in shards:
        steps = jax.random.uniform(jax.random.fold_in(jax.random.fold_in(key, 6), axis_at), (shards_of,), jnp.float32, low / len(shards), largest / len(shards))
        level = level * jnp.repeat(jnp.exp(steps), shape[axis_at] // shards_of).reshape((-1,) + (1,) * (len(shape) - 1 - axis_at))
    return level


def bell_draw(stream_key, extent, spread, bound, cuts=(), kind=jnp.bfloat16):
    array = spread * jax.random.normal(stream_key, extent, jnp.float32)
    if cuts:
        array = array * block_levels(stream_key, extent, cuts, -0.22, 0.18)
    return jnp.clip(array, -bound, bound).astype(kind)


def setup_inputs(seed: int = 0) -> dict:
    arg_keys = jax.random.split(jax.random.key(seed), 4)
    potential = bell_draw(arg_keys[0], (NX, NY, NZ), 0.06, 0.875, ((0, 4), (1, 8)), jnp.float32)
    density = draw_density(jax.random.fold_in(arg_keys[3], 71), 0)
    correction = bell_draw(arg_keys[2], (NX, NY, NZ), 0.5, 6.0, ((0, 4), (1, 8)), jnp.float32)
    return {"potential": potential, "density": density, "correction": correction}


screening = 0.002
damping = 0.6


def roller(values):
    def getter(shift_x, shift_y, shift_z):
        return jnp.roll(values, (-shift_x, -shift_y, -shift_z), axis=(0, 1, 2))
    return getter


def hessian(getter):
    centre = getter(0, 0, 0)

    def second(shift_x, shift_y, shift_z):
        return getter(shift_x, shift_y, shift_z) + getter(-shift_x, -shift_y, -shift_z) - 2.0 * centre

    def cross_term(ax_x, ax_y, ax_z, bx_x, bx_y, bx_z):
        plus_plus = getter(ax_x + bx_x, ax_y + bx_y, ax_z + bx_z)
        plus_minus = getter(ax_x - bx_x, ax_y - bx_y, ax_z - bx_z)
        minus_plus = getter(bx_x - ax_x, bx_y - ax_y, bx_z - ax_z)
        minus_minus = getter(-ax_x - bx_x, -ax_y - bx_y, -ax_z - bx_z)
        return 0.25 * (plus_plus - plus_minus - minus_plus + minus_minus)

    return (second(1, 0, 0), second(0, 1, 0), second(0, 0, 1),
            cross_term(1, 0, 0, 0, 1, 0), cross_term(1, 0, 0, 0, 0, 1), cross_term(0, 1, 0, 0, 0, 1))


def cofactors(hess):
    mat_xx = 1.0 + hess[0]
    mat_yy = 1.0 + hess[1]
    mat_zz = 1.0 + hess[2]
    mat_xy, mat_xz, mat_yz = hess[3], hess[4], hess[5]
    cof_xx = mat_yy * mat_zz - mat_yz * mat_yz
    cof_yy = mat_xx * mat_zz - mat_xz * mat_xz
    cof_zz = mat_xx * mat_yy - mat_xy * mat_xy
    cof_xy = mat_xz * mat_yz - mat_xy * mat_zz
    cof_xz = mat_xy * mat_yz - mat_xz * mat_yy
    cof_yz = mat_xy * mat_xz - mat_xx * mat_yz
    determinant = mat_xx * cof_xx + mat_xy * cof_xy + mat_xz * cof_xz
    return (cof_xx, cof_yy, cof_zz, cof_xy, cof_xz, cof_yz), determinant


def operate(getter, coeffs, spacing):
    centre = getter(0, 0, 0)
    terms = hessian(getter)
    summed = coeffs[0] * terms[0] + coeffs[1] * terms[1] + coeffs[2] * terms[2]
    summed = summed + 2.0 * (coeffs[3] * terms[3] + coeffs[4] * terms[4] + coeffs[5] * terms[5])
    return spacing * summed - screening * centre


def diagonal_of(coeffs, spacing):
    return -2.0 * spacing * (coeffs[0] + coeffs[1] + coeffs[2]) - screening


def relax(estimate, coeffs, diagonal, source, spacing):
    return estimate + damping * (source - operate(roller(estimate), coeffs, spacing)) / diagonal


def block_mean(values):
    size_x, size_y, size_z = values.shape
    shaped = values.reshape(size_x // FACTOR, FACTOR, size_y // FACTOR, FACTOR, size_z // FACTOR, FACTOR)
    return jnp.mean(shaped, axis=(1, 3, 5))


def spread_up(values):
    grown = jnp.repeat(values, FACTOR, axis=0)
    grown = jnp.repeat(grown, FACTOR, axis=1)
    return jnp.repeat(grown, FACTOR, axis=2)


def reference(potential, density, correction):
    coeffs, determinant = cofactors(hessian(roller(potential)))
    source = density - determinant
    diagonal = diagonal_of(coeffs, 1.0)
    estimate = correction
    for counter in range(PRE):
        estimate = relax(estimate, coeffs, diagonal, source, 1.0)
    fine_residual = source - operate(roller(estimate), coeffs, 1.0)
    coarse_source = block_mean(fine_residual)
    coarse_coeffs = tuple(block_mean(entry) for entry in coeffs)
    coarse_spacing = 1.0 / FACTOR ** 2
    coarse_diagonal = diagonal_of(coarse_coeffs, coarse_spacing)
    coarse = jnp.zeros(coarse_source.shape, jnp.float32)
    for counter in range(COARSE_SWEEPS):
        coarse = relax(coarse, coarse_coeffs, coarse_diagonal, coarse_source, coarse_spacing)
    estimate = estimate + spread_up(coarse)
    for counter in range(POST):
        estimate = relax(estimate, coeffs, diagonal, source, 1.0)
    residual = source - operate(roller(estimate), coeffs, 1.0)
    return estimate, residual
```

```python
import functools

import jax
import jax.numpy as jnp
from jax import lax
from jax.experimental import pallas as pl
from jax.experimental.pallas import tpu as pltpu
from jax.sharding import PartitionSpec as P

MESH = pl.DeviceIdType.MESH
SCREEN = 0.002
DAMP = 0.6
UNROLL = {10: 5, 12: 6, 14: 7, 16: 8, 18: 9, 20: 10}
F32 = jnp.float32
NEIGHBOURS = [(-1, -1), (-1, 0), (-1, 1), (0, -1), (0, 1), (1, -1), (1, 0), (1, 1)]
ALONG_X, ALONG_Y, DIAGONAL = [1, 6], [3, 4], [0, 2, 5, 7]
REACH = 3


def x_up(v):
    return jnp.concatenate([v[1:], pltpu.roll(v[0], v.shape[1] - 1, 0)[None]], axis=0)


def x_down(v):
    return jnp.concatenate([pltpu.roll(v[3], 1, 0)[None], v[:3]], axis=0)


def first_plane(load, at):
    v = load(at)
    zp = pltpu.roll(v, v.shape[2] - 1, 2)
    zm = pltpu.roll(v, 1, 2)
    xp, xm = x_up(v), x_down(v)
    dz = zp - zm
    return v, dz, xp - xm, zp + zm, xp + xm, x_up(dz) - x_down(dz)


def walk(load, low, high, emit):
    def step(at, carry):
        before, here = carry
        after = first_plane(load, at + 1)
        emit(
            at,
            here[0],
            here[4],
            before[0] + after[0],
            here[3],
            after[2] - before[2],
            here[5],
            after[1] - before[1],
        )
        return here[:3], after

    carry = (first_plane(load, low - 1)[:3], first_plane(load, low))
    if high - low <= 3:
        for at in range(low, high):
            carry = step(at, carry)
    else:
        lax.fori_loop(low, high, step, carry, unroll=UNROLL.get(high - low, 1))


def dot_exact(values, table):
    hi = values.astype(jnp.bfloat16)
    rest = values - hi.astype(F32)
    mid = rest.astype(jnp.bfloat16)
    lo = (rest - mid.astype(F32)).astype(jnp.bfloat16)
    n = values.shape[0]
    out = jnp.dot(jnp.concatenate([hi, mid, lo], axis=0), table, preferred_element_type=F32)
    return out[:n] + out[n : 2 * n] + out[2 * n :]


def kernel(
    gx_n, gy_n, p_in, d_in, c_in, up_out, res_out,
    pot, cor, den, coef, wgt, src, one, two, fin, up_flat, res_flat,
    pool_c, pool_s, co, cs, wide, grown, back,
    there, sent, got, local,
):
    nx, ny, nz = p_in.shape
    cols = nx // 4 + 2
    y0, y1, x0, x1 = REACH, REACH + ny, 4, 4 + nx
    gx = lax.axis_index("gx")
    gy = lax.axis_index("gy")

    def device(dx, dy):
        return (lax.rem(gx + dx + gx_n, gx_n), lax.rem(gy + dy + gy_n, gy_n))

    barrier = pltpu.get_barrier_semaphore()
    for i in ALONG_X + ALONG_Y:
        pl.semaphore_signal(barrier, inc=1, device_id=device(*NEIGHBOURS[i]), device_id_type=MESH)
    fields = ((p_in, pot, 3), (d_in, den, 2), (c_in, cor, 3))
    for a, b, _ in fields:
        for y in range(ny):
            pltpu.make_async_copy(a.at[:, y], b.at[y0 + y, x0:x1], local.at[0]).start()
    wide[:, :, 14:16, :] = jnp.zeros((7, 3, 2, nz), F32)

    def take(rows, sem):
        ref = coef.reshape(coef.shape[0] * coef.shape[1] * 4 * cols, nz).at[0:rows]
        pltpu.make_async_copy(ref, ref, sem).wait()

    pl.semaphore_wait(barrier, 4)
    for i in ALONG_Y:
        pl.semaphore_signal(there, inc=1, device_id=device(*NEIGHBOURS[i]), device_id_type=MESH)

    def remote(a, b, send, recv, to):
        pltpu.make_async_remote_copy(
            src_ref=a, dst_ref=b, send_sem=send, recv_sem=recv, device_id=device(*to), device_id_type=MESH,
        ).start()

    def send_halo(i, k):
        dx, dy = NEIGHBOURS[i]
        a, b, width = fields[k]
        xs, xd = {1: (nx - width, x0 - width), -1: (0, x1), 0: (0, x0)}[dx]
        ys, yd = {1: (ny - width, y0 - width), -1: (0, y1), 0: (0, y0)}[dy]
        sem = got.at[(1 if k == 2 else 0) + (2 if dy else 0)]
        for r in range(width):
            if dy == 0:
                part, into = a.at[xs + r], b.at[y0:y1, xd + r]
            else:
                n = width if dx else nx
                part, into = a.at[xs : xs + n, ys + r], b.at[yd + r, xd : xd + n]
            remote(part, into, sent.at[0], sem, (dx, dy))

    for where in (ALONG_X, ALONG_Y):
        for k in range(3):
            for i in where:
                send_halo(i, k)
    pl.semaphore_wait(there, 2)
    for k in range(3):
        for i in DIAGONAL:
            send_halo(i, k)
    rows_x = [2 * ny * w for _, _, w in fields]
    rows_y = [2 * nx * w + 4 * w * w for _, _, w in fields]

    rows_at = lax.broadcasted_iota(jnp.int32, (4 * nz, nz), 0)
    cols_at = lax.broadcasted_iota(jnp.int32, (4 * nz, nz), 1)
    group = nz // 4
    mean_table = jnp.where(
        (rows_at // nz) * group + (rows_at % nz) // 4 == cols_at, 1.0 / 64.0, 0.0
    ).astype(jnp.bfloat16)

    def by_rows(ref):
        def load(at):
            return jnp.stack([ref[at, pl.ds(j, cols, stride=4), :] for j in range(4)])

        return load

    def whole(ref):
        def load(at):
            return ref[at]

        return load

    def corrected(at):
        return fin[at] + grown[lax.div(at + 1, 4)][None]

    def build(at, v, xs, ys, zs, dxy, dxz, dyz):
        twice = 2.0 * v
        xx, yy, zz = 1.0 + (xs - twice), 1.0 + (ys - twice), 1.0 + (zs - twice)
        xy, xz, yz = 0.25 * dxy, 0.25 * dxz, 0.25 * dyz
        cxx = yy * zz - yz * yz
        cyy = xx * zz - xz * xz
        czz = xx * yy - xy * xy
        cxy = xz * yz - xy * zz
        cxz = xy * yz - xz * yy
        cyz = xy * xz - xx * yz
        src[at] = by_rows(den)(at) - (xx * cxx + xy * cxy + xz * cxz)
        wgt[at] = DAMP / (-2.0 * (cxx + cyy + czz) - SCREEN)
        coef[0, at], coef[1, at], coef[2, at] = cxx, cyy, czz
        coef[3, at], coef[4, at], coef[5, at] = 0.5 * cxy, 0.5 * cxz, 0.5 * cyz

    def off_diagonal(at, xs, ys, zs, dxy, dxz, dyz):
        return (
            (coef[0, at] * xs + coef[1, at] * ys + coef[2, at] * zs)
            + (coef[3, at] * dxy + coef[4, at] * dxz + coef[5, at] * dyz)
        )

    def relaxed(at, v, *terms):
        return (1.0 - DAMP) * v + wgt[at] * (src[at] - off_diagonal(at, *terms))

    def sweep(load, into, low, high):
        def emit(at, v, *terms):
            into[at] = relaxed(at, v, *terms)

        walk(load, low, high, emit)

    def residual_at(at, v, *terms):
        main = -2.0 * (coef[0, at] + coef[1, at] + coef[2, at]) - SCREEN
        return src[at] - (off_diagonal(at, *terms) + main * v)

    def emit_first(at, v, *terms):
        r = residual_at(at, v, *terms)
        pool_s[at - y0] = (r[0] + r[1]) + (r[2] + r[3])

    def pool_coef(block):
        for f in range(6):
            total = None
            for y in range(4):
                c = coef[f, y0 + 4 * block + y]
                c = (c[0] + c[1]) + (c[2] + c[3])
                total = c if total is None else total + c
            pool_c[block, f] = total

    take(3 * nx * ny, local.at[0])
    take(rows_x[0] + rows_x[1], got.at[0])
    walk(by_rows(pot), y0 + 1, y1 - 1, build)
    take(rows_x[2], got.at[1])
    sweep(by_rows(cor), one, y0 + 1, y1 - 1)
    sweep(whole(one), two, y0 + 2, y1 - 2)
    walk(whole(two), y0 + 3, y1 - 3, emit_first)
    for block in range(1, ny // 4 - 1):
        pool_coef(block)

    take(rows_y[0] + rows_y[1], got.at[2])
    walk(by_rows(pot), y0 - 2, y0 + 1, build)
    walk(by_rows(pot), y1 - 1, y1 + 2, build)
    pool_coef(0)
    pool_coef(ny // 4 - 1)
    parts = [pool_c[block].reshape(6 * cols, nz) for block in range(4)]
    co[...] = dot_exact(jnp.concatenate(parts, axis=1), mean_table).reshape(6, cols, nz)

    def coarse_rows(dx):
        return {1: (slice(3, 7), slice(0, 4)), -1: (slice(1, 5), slice(10, 14)), 0: (slice(1, 7), slice(4, 10))}[dx]

    far_first = (0, 2, 5, 7, 1, 6, 3, 4)
    for i in far_first:
        dx, dy = NEIGHBOURS[i]
        a, b = coarse_rows(dx)
        remote(co.at[:, a], wide.at[0:6, 1 - dy, b], sent.at[1], got.at[4], (dx, dy))

    take(rows_y[2], got.at[3])
    sweep(by_rows(cor), one, y0 - 2, y0 + 1)
    sweep(by_rows(cor), one, y1 - 1, y1 + 2)
    sweep(whole(one), two, y0 - 1, y0 + 2)
    sweep(whole(one), two, y1 - 2, y1 + 1)
    walk(whole(two), y0, y0 + 3, emit_first)
    walk(whole(two), y1 - 3, y1, emit_first)
    parts = [
        (pool_s[4 * b] + pool_s[4 * b + 1]) + (pool_s[4 * b + 2] + pool_s[4 * b + 3]) for b in range(4)
    ]
    cs[...] = dot_exact(jnp.concatenate(parts, axis=1), mean_table)
    for i in far_first:
        dx, dy = NEIGHBOURS[i]
        a, b = coarse_rows(dx)
        remote(cs.at[a], wide.at[6, 1 - dy, b], sent.at[1], got.at[5], (dx, dy))
    for i in far_first:
        dx, dy = NEIGHBOURS[i]
        ys, yd = {
            1: (slice(y1 - REACH, y1), slice(0, y0)),
            -1: (slice(y0, y0 + REACH), slice(y1, y1 + REACH)),
            0: (slice(y0, y1), slice(y0, y1)),
        }[dy]
        if dx == 0:
            a, b = two.at[ys, :, 1 : cols - 1], fin.at[yd, :, 1 : cols - 1]
        elif dx > 0:
            a, b = two.at[ys, 1:4, cols - 2], fin.at[yd, 1:4, 0]
        else:
            a, b = two.at[ys, 0:3, 1], fin.at[yd, 0:3, cols - 1]
        remote(a, b, sent.at[1], got.at[6], (dx, dy))
    rows_c = 6 * (6 * 4 + 2 * 6)
    rows_s = 6 * 4 + 2 * 6
    rows_f = 2 * 3 * ny + 2 * 3 * nx + 4 * 9

    def keep(at, _):
        fin[at, :, 1 : cols - 1, :] = two[at][:, 1 : cols - 1]
        return 0

    lax.fori_loop(y0, y1, keep, 0, unroll=8)
    wide[0:6, 1, 4:10, :] = co[...][:, 1:7]
    wide[6, 1, 4:10, :] = cs[...][1:7]
    rows_b = lax.broadcasted_iota(jnp.int32, (nz, nz), 0)
    cols_b = lax.broadcasted_iota(jnp.int32, (nz, nz), 1)
    for g in range(4):
        back[g] = jnp.where(rows_b == g * group + cols_b // 4, 1.0, 0.0).astype(jnp.bfloat16)
    take(sum(rows_x) + sum(rows_y), sent.at[0])

    take(rows_c, got.at[4])
    cc = [wide[f] for f in range(6)]
    spacing = 1.0 / 16.0
    coarse_w = DAMP / (-2.0 * spacing * (cc[0] + cc[1] + cc[2]) - SCREEN)
    cc = [spacing * c for c in cc]
    take(rows_s, got.at[5])
    coarse_b = wide[6]
    lane = lax.broadcasted_iota(jnp.int32, (3, 16, nz), 2)
    in_group = lane % group

    def y_up(v):
        r = pltpu.roll(v, nz - group, 2)
        return jnp.where(lane < nz - group, r, jnp.concatenate([r[1:], r[:1]], axis=0))

    def y_down(v):
        r = pltpu.roll(v, group, 2)
        return jnp.where(lane >= group, r, jnp.concatenate([r[2:], r[:2]], axis=0))

    value = coarse_w * coarse_b
    for _ in range(3):
        zp = jnp.where(in_group == group - 1, pltpu.roll(value, group - 1, 2), pltpu.roll(value, nz - 1, 2))
        zm = jnp.where(in_group == 0, pltpu.roll(value, nz - group + 1, 2), pltpu.roll(value, 1, 2))
        dz = zp - zm
        yp, ym = y_up(value), y_down(value)
        dy_ = yp - ym
        xs = pltpu.roll(value, 15, 1) + pltpu.roll(value, 1, 1)
        dxy = pltpu.roll(dy_, 15, 1) - pltpu.roll(dy_, 1, 1)
        dxz = pltpu.roll(dz, 15, 1) - pltpu.roll(dz, 1, 1)
        dyz = y_up(dz) - y_down(dz)
        total = cc[0] * xs + cc[1] * (yp + ym) + cc[2] * (zp + zm)
        total = total + (cc[3] * dxy + cc[4] * dxz + cc[5] * dyz)
        value = (1.0 - DAMP) * value + coarse_w * (coarse_b - total)

    value = pltpu.roll(value, 13, 1)[:, 0:cols]
    for j, (blk, g) in enumerate(((0, 3), (1, 0), (1, 1), (1, 2), (1, 3), (2, 0))):
        grown[j] = dot_exact(value[blk], back[g])

    take(rows_f, got.at[6])
    sweep(corrected, one, y0 - 2, y1 + 2)
    take(rows_c + rows_s + rows_f, sent.at[1])

    def rows_of(flat, at, value):
        for j in range(4):
            flat[at, pl.ds(j, cols, stride=4), :] = value[j]

    def emit_two(at, v, *terms):
        two[at] = relaxed(at, v, *terms)

    walk(whole(one), y0 - 1, y1 + 1, emit_two)

    def emit_last(at, v, *terms):
        rows_of(up_flat, at - y0, 0.5 * v)
        rows_of(res_flat, at - y0, 0.5 * residual_at(at, v, *terms))

    walk(whole(two), y0, y1, emit_last)
    for flat, out in ((up_flat, up_out), (res_flat, res_out)):
        for y in range(ny):
            pltpu.make_async_copy(flat.at[y, x0:x1], out.at[:, y], local.at[0]).start()
    take(2 * nx * ny, local.at[0])


def solution(mesh):
    gx_n, gy_n = mesh.shape["gx"], mesh.shape["gy"]

    def shards(potential, density, correction):
        nx, ny, nz = potential.shape
        cols = nx // 4 + 2
        rows = pltpu.VMEM((ny + 2 * REACH, 4 * cols, nz), F32)
        fine = pltpu.VMEM((ny + 2 * REACH, 4, cols, nz), F32)
        flat = pltpu.VMEM((ny, 4 * cols, nz), F32)
        dma = pltpu.SemaphoreType.DMA
        shape = jax.ShapeDtypeStruct(potential.shape, F32)
        updated, residual = pl.pallas_call(
            functools.partial(kernel, gx_n, gy_n),
            out_shape=(shape, shape),
            in_specs=[pl.BlockSpec(memory_space=pl.ANY)] * 3,
            out_specs=[pl.BlockSpec(memory_space=pltpu.VMEM)] * 2,
            scratch_shapes=[
                rows, rows, rows,
                pltpu.VMEM((6, ny + 2 * REACH, 4, cols, nz), F32),
                fine, fine, fine, fine, fine, flat, flat,
                pltpu.VMEM((4, 6, cols, nz), F32), pltpu.VMEM((ny, cols, nz), F32),
                pltpu.VMEM((6, cols, nz), F32), pltpu.VMEM((cols, nz), F32),
                pltpu.VMEM((7, 3, 16, nz), F32), pltpu.VMEM((6, cols, nz), F32),
                pltpu.VMEM((4, nz, nz), jnp.bfloat16),
                pltpu.SemaphoreType.REGULAR, dma((2,)), dma((7,)), dma((1,)),
            ],
            compiler_params=pltpu.CompilerParams(
                collective_id=0, has_side_effects=True, vmem_limit_bytes=40 * 1024 * 1024
            ),
        )(*[
            pltpu.with_memory_space_constraint(v, pltpu.HBM) for v in (potential, density, correction)
        ])
        return 2.0 * updated, 2.0 * residual

    placed = (P("gx", "gy", None),) * 3
    return jax.shard_map(
        shards, mesh=mesh, in_specs=placed,
        out_specs=(P("gx", "gy", None), P("gx", "gy", None)), check_vma=False,
    )
```

```python
import functools

import jax
import jax.numpy as jnp
from jax import lax
from jax.experimental import pallas as pl
from jax.experimental.pallas import tpu as pltpu
from jax.sharding import PartitionSpec as P

MESH = pl.DeviceIdType.MESH
SCREEN = 0.002
DAMP = 0.6
UNROLL = {10: 10, 12: 12, 14: 14, 16: 16, 18: 18, 20: 20}
F32 = jnp.float32
NEIGHBOURS = [(-1, -1), (-1, 0), (-1, 1), (0, -1), (0, 1), (1, -1), (1, 0), (1, 1)]
BESIDE, DIAGONAL = [1, 6, 3, 4], [0, 2, 5, 7]
REACH = 3


def x_up(v):
    return jnp.concatenate([v[1:], pltpu.roll(v[0], v.shape[1] - 1, 0)[None]], axis=0)


def x_down(v):
    return jnp.concatenate([pltpu.roll(v[3], 1, 0)[None], v[:3]], axis=0)


def first_plane(load, at):
    v = load(at)
    zp = pltpu.roll(v, v.shape[2] - 1, 2)
    zm = pltpu.roll(v, 1, 2)
    xp, xm = x_up(v), x_down(v)
    dz = zp - zm
    return v, dz, xp - xm, zp + zm, xp + xm, x_up(dz) - x_down(dz)


def edge(d, width, start, end):
    if d > 0:
        return slice(end - width, end), slice(start - width, start)
    if d < 0:
        return slice(start, start + width), slice(end, end + width)
    return slice(start, end), slice(start, end)


def walk(load, low, high, emit, straight=False):
    def step(at, carry):
        before, here = carry
        after = first_plane(load, at + 1)
        emit(
            at,
            here[0],
            here[4],
            before[0] + after[0],
            here[3],
            after[2] - before[2],
            here[5],
            after[1] - before[1],
        )
        return here[:3], after

    carry = (first_plane(load, low - 1)[:3], first_plane(load, low))
    if straight or high - low <= 3:
        for at in range(low, high):
            carry = step(at, carry)
    else:
        lax.fori_loop(low, high, step, carry, unroll=UNROLL.get(high - low, 1))


def dot_exact(values, table):
    hi = values.astype(jnp.bfloat16)
    rest = values - hi.astype(F32)
    mid = rest.astype(jnp.bfloat16)
    lo = (rest - mid.astype(F32)).astype(jnp.bfloat16)
    n = values.shape[0]
    out = jnp.dot(jnp.concatenate([hi, mid, lo], axis=0), table, preferred_element_type=F32)
    return out[:n] + out[n : 2 * n] + out[2 * n :]


def kernel(
    gx_n, gy_n, p_in, d_in, c_in, up_out, res_out,
    pot, cor, den, coef, wgt, src, one, two, fin, up_flat, res_flat,
    pool_c, pool_s, co, cs, wide, grown, back,
    there, sent, got, local,
):
    nx, ny, nz = p_in.shape
    cols = nx // 4 + 2
    y0, y1, x0, x1 = REACH, REACH + ny, 4, 4 + nx
    gx = lax.axis_index("gx")
    gy = lax.axis_index("gy")

    def device(dx, dy):
        return (lax.rem(gx + dx + gx_n, gx_n), lax.rem(gy + dy + gy_n, gy_n))

    barrier = pltpu.get_barrier_semaphore()
    for i in BESIDE:
        pl.semaphore_signal(barrier, inc=1, device_id=device(*NEIGHBOURS[i]), device_id_type=MESH)
    fields = ((p_in, pot, 3), (d_in, den, 2), (c_in, cor, 3))
    for a, b, _ in fields:
        for y in range(ny):
            pltpu.make_async_copy(a.at[:, y], b.at[y0 + y, x0:x1], local.at[0]).start()
    pl.semaphore_wait(barrier, 4)
    for n, which in enumerate((BESIDE[:2], BESIDE[2:])):
        for i in which:
            pl.semaphore_signal(
                there.at[n], inc=1, device_id=device(*NEIGHBOURS[i]), device_id_type=MESH)

    def take(rows, sem):
        ref = coef.reshape(coef.shape[0] * coef.shape[1] * 4 * cols, nz).at[0:rows]
        pltpu.make_async_copy(ref, ref, sem).wait()

    def remote(a, b, send, recv, to):
        pltpu.make_async_remote_copy(
            src_ref=a, dst_ref=b, send_sem=send, recv_sem=recv, device_id=device(*to), device_id_type=MESH,
        ).start()

    def send_halo(which):
        for k, (_, ref, width) in enumerate(fields):
            for i in which:
                dx, dy = NEIGHBOURS[i]
                part, into = zip(edge(dy, width, y0, y1), edge(dx, width, x0, x1))
                sem = got.at[(1 if k == 2 else 0) + (2 if dy else 0)]
                remote(ref.at[part], ref.at[into], sent.at[0], sem, (dx, dy))

    take(3 * nx * ny, local.at[0])
    send_halo(BESIDE[:2])
    send_halo(BESIDE[2:])
    odd = lax.rem(gy, 2)
    pl.semaphore_wait(there.at[1 - odd], 2)
    send_halo(DIAGONAL)
    pl.semaphore_wait(there.at[odd], 2)
    wide[:, :, 14:16, :] = jnp.zeros((7, 3, 2, nz), F32)
    rows_x = [2 * ny * w for _, _, w in fields]
    rows_y = [2 * nx * w + 4 * w * w for _, _, w in fields]

    rows_at = lax.broadcasted_iota(jnp.int32, (4 * nz, nz), 0)
    cols_at = lax.broadcasted_iota(jnp.int32, (4 * nz, nz), 1)
    group = nz // 4
    mean_table = jnp.where(
        (rows_at // nz) * group + (rows_at % nz) // 4 == cols_at, 1.0 / 64.0, 0.0
    ).astype(jnp.bfloat16)

    def by_rows(ref):
        def load(at):
            return jnp.stack([ref[at, pl.ds(j, cols, stride=4), :] for j in range(4)])

        return load

    def whole(ref):
        def load(at):
            return ref[at]

        return load

    def corrected(at):
        return fin[at] + grown[lax.div(at + 1, 4)][None]

    def build(at, v, xs, ys, zs, dxy, dxz, dyz):
        twice = 2.0 * v
        xx, yy, zz = 1.0 + (xs - twice), 1.0 + (ys - twice), 1.0 + (zs - twice)
        xy, xz, yz = 0.25 * dxy, 0.25 * dxz, 0.25 * dyz
        cxx = yy * zz - yz * yz
        cyy = xx * zz - xz * xz
        czz = xx * yy - xy * xy
        cxy = xz * yz - xy * zz
        cxz = xy * yz - xz * yy
        cyz = xy * xz - xx * yz
        src[at] = by_rows(den)(at) - (xx * cxx + xy * cxy + xz * cxz)
        wgt[at] = DAMP / (-2.0 * (cxx + cyy + czz) - SCREEN)
        coef[0, at], coef[1, at], coef[2, at] = cxx, cyy, czz
        coef[3, at], coef[4, at], coef[5, at] = 0.5 * cxy, 0.5 * cxz, 0.5 * cyz

    def off_diagonal(at, xs, ys, zs, dxy, dxz, dyz):
        return (
            (coef[0, at] * xs + coef[1, at] * ys + coef[2, at] * zs)
            + (coef[3, at] * dxy + coef[4, at] * dxz + coef[5, at] * dyz)
        )

    def relaxed(at, v, *terms):
        return (1.0 - DAMP) * v + wgt[at] * (src[at] - off_diagonal(at, *terms))

    def sweep(load, into, low, high):
        def emit(at, v, *terms):
            into[at] = relaxed(at, v, *terms)

        walk(load, low, high, emit)

    def residual_at(at, v, *terms):
        main = -2.0 * (coef[0, at] + coef[1, at] + coef[2, at]) - SCREEN
        return src[at] - (off_diagonal(at, *terms) + main * v)

    def emit_first(at, v, *terms):
        r = residual_at(at, v, *terms)
        pool_s[at - y0] = (r[0] + r[1]) + (r[2] + r[3])

    def pool_coef(block):
        for f in range(6):
            total = None
            for y in range(4):
                c = coef[f, y0 + 4 * block + y]
                c = (c[0] + c[1]) + (c[2] + c[3])
                total = c if total is None else total + c
            pool_c[block, f] = total

    take(rows_x[0] + rows_x[1], got.at[0])
    walk(by_rows(pot), y0 + 1, y1 - 1, build)
    take(rows_x[2], got.at[1])
    sweep(by_rows(cor), one, y0 + 1, y1 - 1)
    sweep(whole(one), two, y0 + 2, y1 - 2)
    walk(whole(two), y0 + 3, y1 - 3, emit_first)
    for block in range(1, ny // 4 - 1):
        pool_coef(block)

    take(rows_y[0] + rows_y[1], got.at[2])
    walk(by_rows(pot), y0 - 2, y0 + 1, build)
    walk(by_rows(pot), y1 - 1, y1 + 2, build)
    pool_coef(0)
    pool_coef(ny // 4 - 1)
    parts = [pool_c[block].reshape(6 * cols, nz) for block in range(4)]
    co[...] = dot_exact(jnp.concatenate(parts, axis=1), mean_table).reshape(6, cols, nz)

    def coarse_rows(dx):
        return {1: (slice(3, 7), slice(0, 4)), -1: (slice(1, 5), slice(10, 14)), 0: (slice(1, 7), slice(4, 10))}[dx]

    far_first = (0, 2, 5, 7, 1, 6, 3, 4)
    for i in far_first:
        dx, dy = NEIGHBOURS[i]
        a, b = coarse_rows(dx)
        remote(co.at[:, a], wide.at[0:6, 1 - dy, b], sent.at[1], got.at[4], (dx, dy))

    take(rows_y[2], got.at[3])
    sweep(by_rows(cor), one, y0 - 2, y0 + 1)
    sweep(by_rows(cor), one, y1 - 1, y1 + 2)
    sweep(whole(one), two, y0 - 1, y0 + 2)
    sweep(whole(one), two, y1 - 2, y1 + 1)
    walk(whole(two), y0, y0 + 3, emit_first)
    walk(whole(two), y1 - 3, y1, emit_first)
    parts = [
        (pool_s[4 * b] + pool_s[4 * b + 1]) + (pool_s[4 * b + 2] + pool_s[4 * b + 3]) for b in range(4)
    ]
    cs[...] = dot_exact(jnp.concatenate(parts, axis=1), mean_table)
    for i in far_first:
        dx, dy = NEIGHBOURS[i]
        a, b = coarse_rows(dx)
        remote(cs.at[a], wide.at[6, 1 - dy, b], sent.at[1], got.at[5], (dx, dy))
    for i in far_first:
        dx, dy = NEIGHBOURS[i]
        ys, yd = {
            1: (slice(y1 - REACH, y1), slice(0, y0)),
            -1: (slice(y0, y0 + REACH), slice(y1, y1 + REACH)),
            0: (slice(y0, y1), slice(y0, y1)),
        }[dy]
        if dx == 0:
            a, b = two.at[ys, :, 1 : cols - 1], fin.at[yd, :, 1 : cols - 1]
        elif dx > 0:
            a, b = two.at[ys, 1:4, cols - 2], fin.at[yd, 1:4, 0]
        else:
            a, b = two.at[ys, 0:3, 1], fin.at[yd, 0:3, cols - 1]
        remote(a, b, sent.at[1], got.at[6], (dx, dy))
    rows_c = 6 * (6 * 4 + 2 * 6)
    rows_s = 6 * 4 + 2 * 6
    rows_f = 2 * 3 * ny + 2 * 3 * nx + 4 * 9

    def keep(at, _):
        fin[at, :, 1 : cols - 1, :] = two[at][:, 1 : cols - 1]
        return 0

    lax.fori_loop(y0, y1, keep, 0, unroll=8)
    wide[0:6, 1, 4:10, :] = co[...][:, 1:7]
    wide[6, 1, 4:10, :] = cs[...][1:7]
    rows_b = lax.broadcasted_iota(jnp.int32, (nz, nz), 0)
    cols_b = lax.broadcasted_iota(jnp.int32, (nz, nz), 1)
    for g in range(4):
        back[g] = jnp.where(rows_b == g * group + cols_b // 4, 1.0, 0.0).astype(jnp.bfloat16)
    take(sum(rows_x) + sum(rows_y), sent.at[0])

    take(rows_c, got.at[4])
    cc = [wide[f] for f in range(6)]
    spacing = 1.0 / 16.0
    coarse_w = DAMP / (-2.0 * spacing * (cc[0] + cc[1] + cc[2]) - SCREEN)
    cc = [spacing * c for c in cc]
    take(rows_s, got.at[5])
    coarse_b = wide[6]
    lane = lax.broadcasted_iota(jnp.int32, (3, 16, nz), 2)
    in_group = lane % group

    z_end, z_start = in_group == group - 1, in_group == 0

    def y_up(r):
        return jnp.where(lane < nz - group, r, jnp.concatenate([r[1:], r[:1]], axis=0))

    def y_down(r):
        return jnp.where(lane >= group, r, jnp.concatenate([r[2:], r[:2]], axis=0))

    value = coarse_w * coarse_b
    for _ in range(3):
        at = {
            k: pltpu.roll(value, -k % nz, 2)
            for h in (1, group - 1, group, group + 1, 2 * group - 1) for k in (h, -h)
        }
        zp = jnp.where(z_end, at[1 - group], at[1])
        zm = jnp.where(z_start, at[group - 1], at[-1])
        dz = zp - zm
        yp, ym = y_up(at[group]), y_down(at[-group])
        dy_ = yp - ym
        above = jnp.where(z_end, at[1], at[group + 1]) - jnp.where(z_start, at[2 * group - 1], at[group - 1])
        below = jnp.where(z_end, at[1 - 2 * group], at[1 - group]) - jnp.where(z_start, at[-1], at[-group - 1])
        xs = pltpu.roll(value, 15, 1) + pltpu.roll(value, 1, 1)
        dxy = pltpu.roll(dy_, 15, 1) - pltpu.roll(dy_, 1, 1)
        dxz = pltpu.roll(dz, 15, 1) - pltpu.roll(dz, 1, 1)
        dyz = y_up(above) - y_down(below)
        total = cc[0] * xs + cc[1] * (yp + ym) + cc[2] * (zp + zm)
        total = total + (cc[3] * dxy + cc[4] * dxz + cc[5] * dyz)
        value = (1.0 - DAMP) * value + coarse_w * (coarse_b - total)

    value = pltpu.roll(value, 13, 1)[:, 0:cols]
    for j, (blk, g) in enumerate(((0, 3), (1, 0), (1, 1), (1, 2), (1, 3), (2, 0))):
        grown[j] = dot_exact(value[blk], back[g])

    take(rows_f, got.at[6])
    sweep(corrected, one, y0 - 2, y1 + 2)
    take(rows_c + rows_s + rows_f, sent.at[1])

    def rows_of(out, y, value):
        flat = out.reshape(nx * ny, nz)
        for j in range(4):
            flat[pl.ds(j * ny + y, cols - 2, stride=4 * ny), :] = value[j][1 : cols - 1]

    def emit_two(at, v, *terms):
        value = relaxed(at, v, *terms)
        two[at] = value
        if y0 <= at < y1:
            rows_of(up_out, at - y0, 0.5 * value)

    walk(whole(one), y0 - 1, y1 + 1, emit_two, straight=True)

    def emit_last(at, v, *terms):
        rows_of(res_out, at - y0, 0.5 * residual_at(at, v, *terms))

    walk(whole(two), y0, y1, emit_last, straight=True)


def solution(mesh):
    gx_n, gy_n = mesh.shape["gx"], mesh.shape["gy"]

    def shards(potential, density, correction):
        nx, ny, nz = potential.shape
        cols = nx // 4 + 2
        rows = pltpu.VMEM((ny + 2 * REACH, 4 * cols, nz), F32)
        fine = pltpu.VMEM((ny + 2 * REACH, 4, cols, nz), F32)
        dma = pltpu.SemaphoreType.DMA
        shape = jax.ShapeDtypeStruct(potential.shape, F32)
        updated, residual = pl.pallas_call(
            functools.partial(kernel, gx_n, gy_n),
            out_shape=(shape, shape),
            in_specs=[pl.BlockSpec(memory_space=pl.ANY)] * 3,
            out_specs=[pl.BlockSpec(memory_space=pltpu.VMEM)] * 2,
            scratch_shapes=[
                rows, rows, rows,
                pltpu.VMEM((6, ny + 2 * REACH, 4, cols, nz), F32),
                fine, fine, fine, fine, fine,
                pltpu.VMEM((ny + 2, 4 * cols, nz), F32), pltpu.VMEM((ny, 4 * cols, nz), F32),
                pltpu.VMEM((4, 6, cols, nz), F32), pltpu.VMEM((ny, cols, nz), F32),
                pltpu.VMEM((6, cols, nz), F32), pltpu.VMEM((cols, nz), F32),
                pltpu.VMEM((7, 3, 16, nz), F32), pltpu.VMEM((6, cols, nz), F32),
                pltpu.VMEM((4, nz, nz), jnp.bfloat16),
                pltpu.SemaphoreType.REGULAR((2,)), dma((2,)), dma((7,)), dma((1,)),
            ],
            compiler_params=pltpu.CompilerParams(
                collective_id=0, has_side_effects=True, vmem_limit_bytes=40 * 1024 * 1024
            ),
        )(*[
            pltpu.with_memory_space_constraint(v, pltpu.HBM) for v in (potential, density, correction)
        ])
        return 2.0 * updated, 2.0 * residual

    placed = (P("gx", "gy", None),) * 3
    return jax.shard_map(
        shards, mesh=mesh, in_specs=placed,
        out_specs=(P("gx", "gy", None), P("gx", "gy", None)), check_vma=False,
    )
```

```python
import functools

import jax
import jax.numpy as jnp
from jax import lax
from jax.experimental import pallas as pl
from jax.experimental.pallas import tpu as pltpu
from jax.sharding import PartitionSpec as P

MESH = pl.DeviceIdType.MESH
SCREEN = 0.002
DAMP = 0.6
F32 = jnp.float32
NEIGHBOURS = [(-1, -1), (-1, 0), (-1, 1), (0, -1), (0, 1), (1, -1), (1, 0), (1, 1)]
DIAGONAL = [0, 2, 5, 7]
REACH = 3


def x_up(v):
    return jnp.concatenate([v[1:], pltpu.roll(v[0], v.shape[1] - 1, 0)[None]], axis=0)


def x_down(v):
    return jnp.concatenate([pltpu.roll(v[3], 1, 0)[None], v[:3]], axis=0)


def first_plane(load, at):
    v = load(at)
    zp = pltpu.roll(v, v.shape[2] - 1, 2)
    zm = pltpu.roll(v, 1, 2)
    xp, xm = x_up(v), x_down(v)
    dz = zp - zm
    return v, dz, xp - xm, zp + zm, xp + xm, x_up(dz) - x_down(dz)


def edge(d, width, start, end):
    if d > 0:
        return slice(end - width, end), slice(start - width, start)
    if d < 0:
        return slice(start, start + width), slice(end, end + width)
    return slice(start, end), slice(start, end)


def walk(load, low, count, emit, straight=False):
    def step(at, carry):
        before, here = carry
        after = first_plane(load, at + 1)
        emit(
            at,
            here[0],
            here[4],
            before[0] + after[0],
            here[3],
            after[2] - before[2],
            here[5],
            after[1] - before[1],
        )
        return here[:3], after

    carry = (first_plane(load, low - 1)[:3], first_plane(load, low))
    if straight or count <= REACH:
        for k in range(count):
            carry = step(low + k, carry)
    else:
        lax.fori_loop(low, low + count, step, carry, unroll=count)


def dot_exact(values, table):
    hi = values.astype(jnp.bfloat16)
    rest = values - hi.astype(F32)
    mid = rest.astype(jnp.bfloat16)
    lo = (rest - mid.astype(F32)).astype(jnp.bfloat16)
    n = values.shape[0]
    out = jnp.dot(jnp.concatenate([hi, mid, lo], axis=0), table, preferred_element_type=F32)
    return out[:n] + out[n : 2 * n] + out[2 * n :]


def pick(values, lanes):
    return jnp.take_along_axis(values, lanes, axis=1, mode="promise_in_bounds")


def kernel(
    gx_n, gy_n, p_in, d_in, c_in, up_out, res_out,
    pot, cor, den, coef, diag, wgt, src, one, two, fin, up_flat, res_flat,
    pool_c, pool_s, co, cs, wide, grown,
    there, sent, got, local,
):
    nx, ny, nz = p_in.shape
    cols = nx // 4 + 2
    y0, y1, x0, x1 = REACH, REACH + ny, 4, 4 + nx
    gx = lax.axis_index("gx")
    gy = lax.axis_index("gy")

    def device(dx, dy):
        return (lax.rem(gx + dx + gx_n, gx_n), lax.rem(gy + dy + gy_n, gy_n))

    barrier = pltpu.get_barrier_semaphore()
    for i in [1, 6, 3, 4]:
        pl.semaphore_signal(barrier, inc=1, device_id=device(*NEIGHBOURS[i]), device_id_type=MESH)
    fields = ((p_in, pot, 3), (d_in, den, 2), (c_in, cor, 3))
    for a, b, _ in fields:
        for y in range(ny):
            pltpu.make_async_copy(a.at[:, y], b.at[y0 + y, x0:x1], local.at[0]).start()
    pl.semaphore_wait(barrier, 4)
    for n, which in enumerate(([1, 6], [3, 4])):
        for i in which:
            pl.semaphore_signal(
                there.at[n], inc=1, device_id=device(*NEIGHBOURS[i]), device_id_type=MESH)

    def take(rows, sem):
        ref = coef.reshape(coef.shape[0] * coef.shape[1] * 4 * cols, nz).at[0:rows]
        pltpu.make_async_copy(ref, ref, sem).wait()

    def remote(a, b, send, recv, to):
        pltpu.make_async_remote_copy(
            src_ref=a, dst_ref=b, send_sem=send, recv_sem=recv, device_id=device(*to), device_id_type=MESH,
        ).start()

    def send_halo(which):
        for k, (_, ref, width) in enumerate(fields):
            for i in which:
                dx, dy = NEIGHBOURS[i]
                part, into = zip(edge(dy, width, y0, y1), edge(dx, width, x0, x1))
                sem = got.at[k // 2 + {0: 0, -1: 2, 1: 4}[dy]]
                remote(ref.at[part], ref.at[into], sent.at[0], sem, (dx, dy))

    take(3 * nx * ny, local.at[0])
    send_halo([1, 6])
    send_halo([4])
    send_halo([3])
    odd = lax.rem(gy, 2)
    pl.semaphore_wait(there.at[1 - odd], 2)
    send_halo(DIAGONAL)
    pl.semaphore_wait(there.at[odd], 2)
    wide[:, :, 14:16, :] = jnp.zeros((8, 3, 2, nz), F32)
    rows_x = [2 * ny * w for _, _, w in fields]
    rows_y = [nx * w + 2 * w * w for _, _, w in fields]

    rows_at = lax.broadcasted_iota(jnp.int32, (4 * nz, nz), 0)
    cols_at = lax.broadcasted_iota(jnp.int32, (4 * nz, nz), 1)
    group = nz // 4
    mean_table = jnp.where(
        (rows_at // nz) * group + (rows_at % nz) // 4 == cols_at, 1.0 / 64.0, 0.0
    ).astype(jnp.bfloat16)

    lane = lax.broadcasted_iota(jnp.int32, (cols, nz), 1)

    def block_mean(parts):
        at = 4 * (lane % group)
        sums = [(pick(p, at) + pick(p, at + 1)) + (pick(p, at + 2) + pick(p, at + 3)) for p in parts]
        low, high = jnp.where(lane < group, sums[0], sums[1]), jnp.where(lane < 3 * group, sums[2], sums[3])
        return (1.0 / 64.0) * jnp.where(lane < 2 * group, low, high)

    def by_rows(ref):
        def load(at):
            return jnp.stack([ref[at, pl.ds(j, cols, stride=4), :] for j in range(4)])

        return load

    def whole(ref):
        def load(at):
            return ref[at]

        return load

    def corrected(at):
        return fin[at] + grown[lax.div(at + 1, 4)][None]

    def build(at, v, xs, ys, zs, dxy, dxz, dyz):
        twice = 2.0 * v
        xx, yy, zz = 1.0 + (xs - twice), 1.0 + (ys - twice), 1.0 + (zs - twice)
        xy, xz, yz = 0.25 * dxy, 0.25 * dxz, 0.25 * dyz
        cxx = yy * zz - yz * yz
        cyy = xx * zz - xz * xz
        czz = xx * yy - xy * xy
        cxy = xz * yz - xy * zz
        cxz = xy * yz - xz * yy
        cyz = xy * xz - xx * yz
        src[at] = by_rows(den)(at) - (xx * cxx + xy * cxy + xz * cxz)
        main = -2.0 * (cxx + cyy + czz) - SCREEN
        diag[at], wgt[at] = main, DAMP / main
        coef[0, at], coef[1, at], coef[2, at] = cxx, cyy, czz
        coef[3, at], coef[4, at], coef[5, at] = 0.5 * cxy, 0.5 * cxz, 0.5 * cyz

    def off_diagonal(at, xs, ys, zs, dxy, dxz, dyz):
        return (
            (coef[0, at] * xs + coef[1, at] * ys + coef[2, at] * zs)
            + (coef[3, at] * dxy + coef[4, at] * dxz + coef[5, at] * dyz)
        )

    def relaxed(at, v, *terms):
        return (1.0 - DAMP) * v + wgt[at] * (src[at] - off_diagonal(at, *terms))

    def sweep(load, into, low, count):
        def emit(at, v, *terms):
            into[at] = relaxed(at, v, *terms)

        walk(load, low, count, emit)

    def residual_at(at, v, *terms):
        return src[at] - (off_diagonal(at, *terms) + diag[at] * v)

    def emit_first(at, v, *terms):
        r = residual_at(at, v, *terms)
        pool_s[at - y0] = (r[0] + r[1]) + (r[2] + r[3])

    def pool_coef(block, planes, more):
        for f in range(6):
            total = pool_c[block, f] if more else None
            for y in planes:
                c = coef[f, y0 + 4 * block + y]
                c = (c[0] + c[1]) + (c[2] + c[3])
                total = c if total is None else total + c
            pool_c[block, f] = total

    def coarse_rows(dx, reach):
        if dx > 0:
            return slice(7 - reach, 7), slice(4 - reach, 4)
        if dx < 0:
            return slice(1, 1 + reach), slice(10, 10 + reach)
        return slice(1, 7), slice(4, 10)

    take(rows_x[0] + rows_x[1], got.at[0])
    walk(by_rows(pot), y0 + 1, ny - 2, build)
    take(rows_x[2], got.at[1])
    sweep(by_rows(cor), one, y0 + 1, ny - 2)
    sweep(whole(one), two, y0 + 2, ny - 4)
    walk(whole(two), y0 + 3, ny - 6, emit_first)
    for block, planes in enumerate(((1, 2, 3), range(4), range(4), (0, 1, 2))):
        pool_coef(block, planes, False)

    for high in (0, 1):
        take(rows_y[0] + rows_y[1], got.at[4 - 2 * high])
    for high in (0, 1):
        walk(by_rows(pot), y0 - 2 + high * (ny + 1), 3, build)
    pool_coef(0, (0,), True)
    pool_coef(3, (3,), True)
    parts = [pool_c[block].reshape(6 * cols, nz) for block in range(4)]
    means = dot_exact(jnp.concatenate(parts, axis=1), mean_table).reshape(6, cols, nz)
    co[0:6] = means
    co[6] = means[0] + means[1] + means[2]
    far_first = (0, 2, 5, 7, 1, 6, 3, 4)
    for i in far_first:
        dx, dy = NEIGHBOURS[i]
        a, b = coarse_rows(dx, 3)
        remote(co.at[0:6, a], wide.at[0:6, 1 - dy, b], sent.at[1], got.at[6], (dx, dy))
        if dx:
            a, b = (slice(3, 4), slice(0, 1)) if dx > 0 else (slice(4, 5), slice(13, 14))
            remote(co.at[6, a], wide.at[7, 1 - dy, b], sent.at[1], got.at[6], (dx, dy))

    for high in (0, 1):
        take(rows_y[2], got.at[5 - 2 * high])
    for high in (0, 1):
        sweep(by_rows(cor), one, y0 - 2 + high * (ny + 1), 3)
    for high in (0, 1):
        sweep(whole(one), two, y0 - 1 + high * (ny - 1), 3)
    for high in (0, 1):
        walk(whole(two), y0 + high * (ny - 3), 3, emit_first)
    parts = [
        (pool_s[4 * b] + pool_s[4 * b + 1]) + (pool_s[4 * b + 2] + pool_s[4 * b + 3]) for b in range(4)
    ]
    cs[...] = block_mean(parts)
    for i in far_first:
        dx, dy = NEIGHBOURS[i]
        a, b = coarse_rows(dx, 4)
        remote(cs.at[a], wide.at[6, 1 - dy, b], sent.at[1], got.at[7], (dx, dy))
    for i in far_first:
        dx, dy = NEIGHBOURS[i]
        if dx == 0:
            ys, yd = (slice(y1 - 3, y1 - 1), slice(0, 2)) if dy > 0 else (slice(y0 + 1, y0 + 3), slice(y1 + 1, y1 + 3))
            a, b = two.at[ys, :, 1 : cols - 1], fin.at[yd, :, 1 : cols - 1]
        else:
            ys, yd = edge(dy, 3, y0, y1)
            js = slice(1, 3) if dy == 0 else slice(1, 4) if dx > 0 else slice(0, 3)
            s, t = (cols - 2, 0) if dx > 0 else (1, cols - 1)
            a, b = two.at[ys, js, s], fin.at[yd, js, t]
        remote(a, b, sent.at[1], got.at[8], (dx, dy))
    rows_c = 6 * (6 * 3 + 1) + 2 * 6 * 6
    rows_s = 6 * 4 + 2 * 6
    rows_f = 2 * 2 * ny + 2 * 2 * nx + 4 * 9

    def keep(at, _):
        v = two[at]
        fin[at, 0, 1:cols, :] = v[0, 1:cols]
        fin[at, 1:3, 1 : cols - 1, :] = v[1:3, 1 : cols - 1]
        fin[at, 3, 0 : cols - 1, :] = v[3, 0 : cols - 1]
        return 0

    lax.fori_loop(y0, y1, keep, 0, unroll=8)
    for at in (y0 - 1, y1):
        fin[at, :, 1 : cols - 1, :] = two[at][:, 1 : cols - 1]
    wide[0:6, 1, 4:10, :] = co[0:6][:, 1:7]
    wide[6, 1, 4:10, :] = cs[...][1:7]
    take(sum(rows_x) + 2 * sum(rows_y), sent.at[0])

    take(rows_c, got.at[6])
    cc = [wide[f] for f in range(6)]
    spacing = 1.0 / 16.0
    outer = lax.broadcasted_iota(jnp.int32, (3, 16, nz), 1) % 13 == 0
    coarse_w = DAMP / (-2.0 * spacing * jnp.where(outer, wide[7], cc[0] + cc[1] + cc[2]) - SCREEN)
    cc = [spacing * c for c in cc]
    take(rows_s, got.at[7])
    coarse_b = wide[6]
    lane_3 = lax.broadcasted_iota(jnp.int32, (3, 16, nz), 2)
    in_group = lane_3 % group

    z_end, z_start = in_group == group - 1, in_group == 0

    def y_up(r):
        return jnp.where(lane_3 < nz - group, r, jnp.concatenate([r[1:], r[:1]], axis=0))

    def y_down(r):
        return jnp.where(lane_3 >= group, r, jnp.concatenate([r[2:], r[:2]], axis=0))

    value = coarse_w * coarse_b
    for _ in range(3):
        at = {
            k: pltpu.roll(value, -k % nz, 2)
            for h in (1, group - 1, group, group + 1, 2 * group - 1) for k in (h, -h)
        }
        zp = jnp.where(z_end, at[1 - group], at[1])
        zm = jnp.where(z_start, at[group - 1], at[-1])
        dz = zp - zm
        yp, ym = y_up(at[group]), y_down(at[-group])
        dy_ = yp - ym
        above = jnp.where(z_end, at[1], at[group + 1]) - jnp.where(z_start, at[2 * group - 1], at[group - 1])
        below = jnp.where(z_end, at[1 - 2 * group], at[1 - group]) - jnp.where(z_start, at[-1], at[-group - 1])
        xs = pltpu.roll(value, 15, 1) + pltpu.roll(value, 1, 1)
        dxy = pltpu.roll(dy_, 15, 1) - pltpu.roll(dy_, 1, 1)
        dxz = pltpu.roll(dz, 15, 1) - pltpu.roll(dz, 1, 1)
        dyz = y_up(above) - y_down(below)
        total = cc[0] * xs + cc[1] * (yp + ym) + cc[2] * (zp + zm)
        total = total + (cc[3] * dxy + cc[4] * dxz + cc[5] * dyz)
        value = (1.0 - DAMP) * value + coarse_w * (coarse_b - total)

    value = pltpu.roll(value, 13, 1)[:, 0:cols]
    for j, (blk, g) in enumerate(((0, 3), (1, 0), (1, 1), (1, 2), (1, 3), (2, 0))):
        grown[j] = pick(value[blk], g * group + lane // 4)

    take(rows_f, got.at[8])
    sweep(corrected, one, y0 - 2, ny + 4)
    take(rows_c + rows_s + rows_f, sent.at[1])

    def rows_of(out, y, value):
        flat = out.reshape(nx * ny, nz)
        for j in range(4):
            flat[pl.ds(j * ny + y, cols - 2, stride=4 * ny), :] = value[j][1 : cols - 1]

    def emit_two(at, v, *terms):
        value = relaxed(at, v, *terms)
        two[at] = value
        if y0 <= at < y1:
            rows_of(up_out, at - y0, 0.5 * value)

    walk(whole(one), y0 - 1, ny + 2, emit_two, straight=True)

    def emit_last(at, v, *terms):
        rows_of(res_out, at - y0, 0.5 * residual_at(at, v, *terms))

    walk(whole(two), y0, ny, emit_last, straight=True)


def solution(mesh):
    gx_n, gy_n = mesh.shape["gx"], mesh.shape["gy"]

    def shards(potential, density, correction):
        nx, ny, nz = potential.shape
        cols = nx // 4 + 2
        rows = pltpu.VMEM((ny + 2 * REACH, 4 * cols, nz), F32)
        fine = pltpu.VMEM((ny + 2 * REACH, 4, cols, nz), F32)
        dma = pltpu.SemaphoreType.DMA
        shape = jax.ShapeDtypeStruct(potential.shape, F32)
        updated, residual = pl.pallas_call(
            functools.partial(kernel, gx_n, gy_n),
            out_shape=(shape, shape),
            in_specs=[pl.BlockSpec(memory_space=pl.ANY)] * 3,
            out_specs=[pl.BlockSpec(memory_space=pltpu.VMEM)] * 2,
            scratch_shapes=[
                rows, rows, rows,
                pltpu.VMEM((6, ny + 2 * REACH, 4, cols, nz), F32),
                fine, fine, fine, fine, fine, fine,
                pltpu.VMEM((ny + 2, 4 * cols, nz), F32), pltpu.VMEM((ny, 4 * cols, nz), F32),
                pltpu.VMEM((4, 6, cols, nz), F32), pltpu.VMEM((ny, cols, nz), F32),
                pltpu.VMEM((7, cols, nz), F32), pltpu.VMEM((cols, nz), F32),
                pltpu.VMEM((8, 3, 16, nz), F32), pltpu.VMEM((6, cols, nz), F32),
                pltpu.SemaphoreType.REGULAR((3,)), dma((2,)), dma((9,)), dma((1,)),
            ],
            compiler_params=pltpu.CompilerParams(
                collective_id=0, has_side_effects=True, vmem_limit_bytes=40 * 1024 * 1024
            ),
        )(*[
            pltpu.with_memory_space_constraint(v, pltpu.HBM) for v in (potential, density, correction)
        ])
        return 2.0 * updated, 2.0 * residual

    placed = (P("gx", "gy", None),) * 3
    return jax.shard_map(
        shards, mesh=mesh, in_specs=placed,
        out_specs=(P("gx", "gy", None), P("gx", "gy", None)), check_vma=False,
    )
```

```python
import functools

import jax
import jax.numpy as jnp
from jax import lax
from jax.experimental import pallas as pl
from jax.experimental.pallas import tpu as pltpu
from jax.sharding import PartitionSpec as P

MESH = pl.DeviceIdType.MESH
SCREEN = 0.002
DAMP = 0.6
F32 = jnp.float32
NEIGHBOURS = [(-1, -1), (-1, 0), (-1, 1), (0, -1), (0, 1), (1, -1), (1, 0), (1, 1)]
DIAGONAL = [0, 2, 5, 7]
REACH = 3


def x_up(v):
    return jnp.concatenate([v[1:], pltpu.roll(v[0], v.shape[1] - 1, 0)[None]], axis=0)


def x_down(v):
    return jnp.concatenate([pltpu.roll(v[3], 1, 0)[None], v[:3]], axis=0)


def first_plane(load, at):
    v = load(at)
    zp = pltpu.roll(v, v.shape[2] - 1, 2)
    zm = pltpu.roll(v, 1, 2)
    xp, xm = x_up(v), x_down(v)
    dz = zp - zm
    return v, dz, xp - xm, zp + zm, xp + xm, x_up(dz) - x_down(dz)


def edge(d, width, start, end):
    if d > 0:
        return slice(end - width, end), slice(start - width, start)
    if d < 0:
        return slice(start, start + width), slice(end, end + width)
    return slice(start, end), slice(start, end)


def walk(load, low, count, emit, straight=False):
    def step(at, carry):
        before, here = carry
        after = first_plane(load, at + 1)
        emit(
            at,
            here[0],
            here[4],
            before[0] + after[0],
            here[3],
            after[2] - before[2],
            here[5],
            after[1] - before[1],
        )
        return here[:3], after

    carry = (first_plane(load, low - 1)[:3], first_plane(load, low))
    if straight or count <= REACH:
        for k in range(count):
            carry = step(low + k, carry)
    else:
        lax.fori_loop(low, low + count, step, carry, unroll=count)


def dot_exact(values, table):
    hi = values.astype(jnp.bfloat16)
    rest = values - hi.astype(F32)
    mid = rest.astype(jnp.bfloat16)
    lo = (rest - mid.astype(F32)).astype(jnp.bfloat16)
    n = values.shape[0]
    out = jnp.dot(jnp.concatenate([hi, mid, lo], axis=0), table, preferred_element_type=F32)
    return out[:n] + out[n : 2 * n] + out[2 * n :]


def pick(values, lanes):
    return jnp.take_along_axis(values, lanes, axis=1, mode="promise_in_bounds")


def off_diagonal(coef, at, xs, ys, zs, dxy, dxz, dyz):
    return (
        (coef[0, at] * xs + coef[1, at] * ys + coef[2, at] * zs)
        + (coef[3, at] * dxy + coef[4, at] * dxz + coef[5, at] * dyz)
    )


def whole(ref):
    def load(at):
        return ref[at]

    return load


def relaxed(fields, at, v, *terms):
    coef, src, wgt = fields
    return (1.0 - DAMP) * v + wgt[at] * (src[at] - off_diagonal(coef, at, *terms))


def finish(one, coef, src, diag, wgt, up_out, res_out, two, up, res, sem):
    nx, ny, nz = up_out.shape
    cells = nx // 4

    def rows_of(out, y, value):
        flat = out.reshape(nx * ny, nz)
        for j in range(4):
            flat[pl.ds(j * ny + y, cells, stride=4 * ny), :] = value[j][1 : 1 + cells]

    def emit_two(at, v, *terms):
        value = relaxed((coef, src, wgt), at, v, *terms)
        two[at] = value
        if REACH <= at < REACH + ny:
            rows_of(up, at - REACH, value)

    walk(whole(one), REACH - 1, ny + 2, emit_two, straight=True)
    copies = [pltpu.make_async_copy(up, up_out, sem.at[0])]
    copies[0].start()

    def emit_last(at, v, *terms):
        rows_of(res, at - REACH, src[at] - (off_diagonal(coef, at, *terms) + diag[at] * v))

    half = ny // 2
    for n in range(2):
        rows = slice(n * half, (n + 1) * half)
        walk(whole(two), REACH + n * half, half, emit_last, straight=True)
        copies.append(pltpu.make_async_copy(res.at[:, rows], res_out.at[:, rows], sem.at[n + 1]))
        copies[-1].start()
    for copy in copies:
        copy.wait()


def kernel(
    gx_n, gy_n, p_in, d_in, c_in, one, coef, src, diag, wgt,
    pot, cor, den, two, fin,
    pool_c, pool_s, co, cs, wide, grown,
    there, sent, got, local,
):
    nx, ny, nz = p_in.shape
    cols = nx // 4 + 2
    y0, y1, x0, x1 = REACH, REACH + ny, 4, 4 + nx
    gx = lax.axis_index("gx")
    gy = lax.axis_index("gy")

    def device(dx, dy):
        return (lax.rem(gx + dx + gx_n, gx_n), lax.rem(gy + dy + gy_n, gy_n))

    barrier = pltpu.get_barrier_semaphore()
    for i in [1, 6, 3, 4]:
        pl.semaphore_signal(barrier, inc=1, device_id=device(*NEIGHBOURS[i]), device_id_type=MESH)
    fields = ((p_in, pot, 3), (d_in, den, 2), (c_in, cor, 3))
    for a, b, _ in fields:
        for y in range(ny):
            pltpu.make_async_copy(a.at[:, y], b.at[y0 + y, x0:x1], local.at[0]).start()
    pl.semaphore_wait(barrier, 4)
    for n, which in enumerate(([1, 6], [3, 4])):
        for i in which:
            pl.semaphore_signal(
                there.at[n], inc=1, device_id=device(*NEIGHBOURS[i]), device_id_type=MESH)

    def take(rows, sem):
        ref = coef.reshape(coef.shape[0] * coef.shape[1] * 4 * cols, nz).at[0:rows]
        pltpu.make_async_copy(ref, ref, sem).wait()

    def remote(a, b, send, recv, to):
        pltpu.make_async_remote_copy(
            src_ref=a, dst_ref=b, send_sem=send, recv_sem=recv, device_id=device(*to), device_id_type=MESH,
        ).start()

    def send_halo(which):
        for k, (_, ref, width) in enumerate(fields):
            for i in which:
                dx, dy = NEIGHBOURS[i]
                part, into = zip(edge(dy, width, y0, y1), edge(dx, width, x0, x1))
                sem = got.at[k // 2 + (2 if dy else 0)]
                remote(ref.at[part], ref.at[into], sent.at[0], sem, (dx, dy))

    take(3 * nx * ny, local.at[0])
    send_halo([1, 6])
    send_halo([4])
    send_halo([3])
    odd = lax.rem(gy, 2)
    pl.semaphore_wait(there.at[1 - odd], 2)
    send_halo(DIAGONAL)
    pl.semaphore_wait(there.at[odd], 2)
    wide[:, :, 14:16, :] = jnp.zeros((8, 3, 2, nz), F32)
    rows_x = [2 * ny * w for _, _, w in fields]
    rows_y = [nx * w + 2 * w * w for _, _, w in fields]

    rows_at = lax.broadcasted_iota(jnp.int32, (4 * nz, nz), 0)
    cols_at = lax.broadcasted_iota(jnp.int32, (4 * nz, nz), 1)
    group = nz // 4
    mean_table = jnp.where(
        (rows_at // nz) * group + (rows_at % nz) // 4 == cols_at, 1.0 / 64.0, 0.0
    ).astype(jnp.bfloat16)

    lane = lax.broadcasted_iota(jnp.int32, (cols, nz), 1)

    def block_mean(parts):
        at = 4 * (lane % group)
        sums = [(pick(p, at) + pick(p, at + 1)) + (pick(p, at + 2) + pick(p, at + 3)) for p in parts]
        low, high = jnp.where(lane < group, sums[0], sums[1]), jnp.where(lane < 3 * group, sums[2], sums[3])
        return (1.0 / 64.0) * jnp.where(lane < 2 * group, low, high)

    def by_rows(ref):
        def load(at):
            return jnp.stack([ref[at, pl.ds(j, cols, stride=4), :] for j in range(4)])

        return load

    def corrected(at):
        return fin[at] + grown[lax.div(at + 1, 4)][None]

    def build(at, v, xs, ys, zs, dxy, dxz, dyz):
        twice = 2.0 * v
        xx, yy, zz = 1.0 + (xs - twice), 1.0 + (ys - twice), 1.0 + (zs - twice)
        xy, xz, yz = 0.25 * dxy, 0.25 * dxz, 0.25 * dyz
        cxx = yy * zz - yz * yz
        cyy = xx * zz - xz * xz
        czz = xx * yy - xy * xy
        cxy = xz * yz - xy * zz
        cxz = xy * yz - xz * yy
        cyz = xy * xz - xx * yz
        src[at] = by_rows(den)(at) - (xx * cxx + xy * cxy + xz * cxz)
        main = -2.0 * (cxx + cyy + czz) - SCREEN
        diag[at], wgt[at] = main, DAMP / main
        coef[0, at], coef[1, at], coef[2, at] = cxx, cyy, czz
        coef[3, at], coef[4, at], coef[5, at] = 0.5 * cxy, 0.5 * cxz, 0.5 * cyz

    def sweep(load, into, low, count):
        def emit(at, v, *terms):
            into[at] = relaxed((coef, src, wgt), at, v, *terms)

        walk(load, low, count, emit)

    def residual_at(at, v, *terms):
        return src[at] - (off_diagonal(coef, at, *terms) + diag[at] * v)

    def emit_first(at, v, *terms):
        r = residual_at(at, v, *terms)
        pool_s[at - y0] = (r[0] + r[1]) + (r[2] + r[3])

    def pool_coef(block, planes, more):
        for f in range(6):
            total = pool_c[block, f] if more else None
            for y in planes:
                c = coef[f, y0 + 4 * block + y]
                c = (c[0] + c[1]) + (c[2] + c[3])
                total = c if total is None else total + c
            pool_c[block, f] = total

    def coarse_rows(dx, reach):
        if dx > 0:
            return slice(7 - reach, 7), slice(4 - reach, 4)
        if dx < 0:
            return slice(1, 1 + reach), slice(10, 10 + reach)
        return slice(1, 7), slice(4, 10)

    take(rows_x[0] + rows_x[1], got.at[0])
    walk(by_rows(pot), y0 + 1, ny - 2, build)
    take(rows_x[2], got.at[1])
    sweep(by_rows(cor), one, y0 + 1, ny - 2)
    sweep(whole(one), two, y0 + 2, ny - 4)
    walk(whole(two), y0 + 3, ny - 6, emit_first)
    for block, planes in enumerate(((1, 2, 3), range(4), range(4), (0, 1, 2))):
        pool_coef(block, planes, False)

    take(2 * (rows_y[0] + rows_y[1]), got.at[2])
    for high in (0, 1):
        walk(by_rows(pot), y0 - 2 + high * (ny + 1), 3, build)
    pool_coef(0, (0,), True)
    pool_coef(3, (3,), True)
    parts = [pool_c[block].reshape(6 * cols, nz) for block in range(4)]
    means = dot_exact(jnp.concatenate(parts, axis=1), mean_table).reshape(6, cols, nz)
    co[0:6] = means
    co[6] = means[0] + means[1] + means[2]
    far_first = (0, 2, 5, 7, 1, 6, 3, 4)
    for i in far_first:
        dx, dy = NEIGHBOURS[i]
        a, b = coarse_rows(dx, 3)
        remote(co.at[0:6, a], wide.at[0:6, 1 - dy, b], sent.at[0], got.at[4], (dx, dy))
        if dx:
            a, b = (slice(3, 4), slice(0, 1)) if dx > 0 else (slice(4, 5), slice(13, 14))
            remote(co.at[6, a], wide.at[7, 1 - dy, b], sent.at[0], got.at[4], (dx, dy))

    take(2 * rows_y[2], got.at[3])
    for high in (0, 1):
        sweep(by_rows(cor), one, y0 - 2 + high * (ny + 1), 3)
    for high in (0, 1):
        sweep(whole(one), two, y0 - 1 + high * (ny - 1), 3)
    for high in (0, 1):
        walk(whole(two), y0 + high * (ny - 3), 3, emit_first)
    parts = [
        (pool_s[4 * b] + pool_s[4 * b + 1]) + (pool_s[4 * b + 2] + pool_s[4 * b + 3]) for b in range(4)
    ]
    cs[...] = block_mean(parts)
    for i in far_first:
        dx, dy = NEIGHBOURS[i]
        a, b = coarse_rows(dx, 4)
        remote(cs.at[a], wide.at[6, 1 - dy, b], sent.at[0], got.at[5], (dx, dy))
    for i in far_first:
        dx, dy = NEIGHBOURS[i]
        if dx == 0:
            ys, yd = (slice(y1 - 3, y1 - 1), slice(0, 2)) if dy > 0 else (slice(y0 + 1, y0 + 3), slice(y1 + 1, y1 + 3))
            a, b = two.at[ys, :, 1 : cols - 1], fin.at[yd, :, 1 : cols - 1]
        else:
            ys, yd = edge(dy, 3, y0, y1)
            js = slice(1, 3) if dy == 0 else slice(1, 4) if dx > 0 else slice(0, 3)
            s, t = (cols - 2, 0) if dx > 0 else (1, cols - 1)
            a, b = two.at[ys, js, s], fin.at[yd, js, t]
        remote(a, b, sent.at[0], got.at[6], (dx, dy))
    rows_c = 6 * (6 * 3 + 1) + 2 * 6 * 6
    rows_s = 6 * 4 + 2 * 6
    rows_f = 2 * 2 * ny + 2 * 2 * nx + 4 * 9

    def keep(at, _):
        v = two[at]
        fin[at, 0, 1:cols, :] = v[0, 1:cols]
        fin[at, 1:3, 1 : cols - 1, :] = v[1:3, 1 : cols - 1]
        fin[at, 3, 0 : cols - 1, :] = v[3, 0 : cols - 1]
        return 0

    lax.fori_loop(y0, y1, keep, 0, unroll=8)
    for at in (y0 - 1, y1):
        fin[at, :, 1 : cols - 1, :] = two[at][:, 1 : cols - 1]
    wide[0:6, 1, 4:10, :] = co[0:6][:, 1:7]
    wide[6, 1, 4:10, :] = cs[...][1:7]

    take(rows_c, got.at[4])
    cc = [wide[f] for f in range(6)]
    spacing = 1.0 / 16.0
    outer = lax.broadcasted_iota(jnp.int32, (3, 16, nz), 1) % 13 == 0
    coarse_w = DAMP / (-2.0 * spacing * jnp.where(outer, wide[7], cc[0] + cc[1] + cc[2]) - SCREEN)
    cc = [spacing * c for c in cc]
    take(rows_s, got.at[5])
    coarse_b = wide[6]
    lane_3 = lax.broadcasted_iota(jnp.int32, (3, 16, nz), 2)
    in_group = lane_3 % group

    z_end, z_start = in_group == group - 1, in_group == 0

    def y_up(r):
        return jnp.where(lane_3 < nz - group, r, jnp.concatenate([r[1:], r[:1]], axis=0))

    def y_down(r):
        return jnp.where(lane_3 >= group, r, jnp.concatenate([r[2:], r[:2]], axis=0))

    value = coarse_w * coarse_b
    for _ in range(3):
        at = {
            k: pltpu.roll(value, -k % nz, 2)
            for h in (1, group - 1, group, group + 1, 2 * group - 1) for k in (h, -h)
        }
        zp = jnp.where(z_end, at[1 - group], at[1])
        zm = jnp.where(z_start, at[group - 1], at[-1])
        dz = zp - zm
        yp, ym = y_up(at[group]), y_down(at[-group])
        dy_ = yp - ym
        above = jnp.where(z_end, at[1], at[group + 1]) - jnp.where(z_start, at[2 * group - 1], at[group - 1])
        below = jnp.where(z_end, at[1 - 2 * group], at[1 - group]) - jnp.where(z_start, at[-1], at[-group - 1])
        xs = pltpu.roll(value, 15, 1) + pltpu.roll(value, 1, 1)
        dxy = pltpu.roll(dy_, 15, 1) - pltpu.roll(dy_, 1, 1)
        dxz = pltpu.roll(dz, 15, 1) - pltpu.roll(dz, 1, 1)
        dyz = y_up(above) - y_down(below)
        total = cc[0] * xs + cc[1] * (yp + ym) + cc[2] * (zp + zm)
        total = total + (cc[3] * dxy + cc[4] * dxz + cc[5] * dyz)
        value = (1.0 - DAMP) * value + coarse_w * (coarse_b - total)

    value = pltpu.roll(value, 13, 1)[:, 0:cols]
    for j, (blk, g) in enumerate(((0, 3), (1, 0), (1, 1), (1, 2), (1, 3), (2, 0))):
        grown[j] = pick(value[blk], g * group + lane // 4)

    take(rows_f, got.at[6])
    sweep(corrected, one, y0 - 2, ny + 4)
    take(sum(rows_x) + 2 * sum(rows_y) + rows_c + rows_s + rows_f, sent.at[0])


def solution(mesh):
    gx_n, gy_n = mesh.shape["gx"], mesh.shape["gy"]

    def shards(potential, density, correction):
        nx, ny, nz = potential.shape
        cols = nx // 4 + 2
        rows = pltpu.VMEM((ny + 2 * REACH, 4 * cols, nz), F32)
        fine = pltpu.VMEM((ny + 2 * REACH, 4, cols, nz), F32)
        dma = pltpu.SemaphoreType.DMA
        field = (ny + 2 * REACH, 4, cols, nz)
        shape = jax.ShapeDtypeStruct(potential.shape, F32)
        fields = [jax.ShapeDtypeStruct(s, F32) for s in (field, (6, *field), field, field, field)]
        vmem, hbm = pl.BlockSpec(memory_space=pltpu.VMEM), pl.BlockSpec(memory_space=pltpu.HBM)
        parts = pl.pallas_call(
            functools.partial(kernel, gx_n, gy_n),
            out_shape=tuple(fields),
            in_specs=[pl.BlockSpec(memory_space=pl.ANY)] * 3,
            out_specs=[vmem] * 5,
            scratch_shapes=[
                rows, rows, rows, fine, fine,
                pltpu.VMEM((4, 6, cols, nz), F32), pltpu.VMEM((ny, cols, nz), F32),
                pltpu.VMEM((7, cols, nz), F32), pltpu.VMEM((cols, nz), F32),
                pltpu.VMEM((8, 3, 16, nz), F32), pltpu.VMEM((6, cols, nz), F32),
                pltpu.SemaphoreType.REGULAR((2,)), dma((1,)), dma((7,)), dma((1,)),
            ],
            compiler_params=pltpu.CompilerParams(
                collective_id=0, has_side_effects=True, vmem_limit_bytes=30 * 1024 * 1024
            ),
        )(*[
            pltpu.with_memory_space_constraint(v, pltpu.HBM) for v in (potential, density, correction)
        ])
        return pl.pallas_call(
            finish,
            out_shape=(shape, shape),
            in_specs=[vmem] * 5,
            out_specs=[hbm] * 2,
            scratch_shapes=[fine, pltpu.VMEM(potential.shape, F32), pltpu.VMEM(potential.shape, F32), dma((3,))],
            compiler_params=pltpu.CompilerParams(vmem_limit_bytes=20 * 1024 * 1024),
        )(*parts)

    placed = (P("gx", "gy", None),) * 3
    return jax.shard_map(
        shards, mesh=mesh, in_specs=placed,
        out_specs=(P("gx", "gy", None), P("gx", "gy", None)), check_vma=False,
    )
```

```python
import functools

import jax
import jax.numpy as jnp
from jax import lax
from jax.experimental import pallas as pl
from jax.experimental.pallas import tpu as pltpu
from jax.sharding import PartitionSpec as P

MESH = pl.DeviceIdType.MESH
SCREEN = 0.002
DAMP = 0.6
F32 = jnp.float32
NEIGHBOURS = [(-1, -1), (-1, 0), (-1, 1), (0, -1), (0, 1), (1, -1), (1, 0), (1, 1)]
DIAGONAL = [0, 2, 5, 7]
REACH = 3


def x_up(v):
    return jnp.concatenate([v[1:], pltpu.roll(v[0], v.shape[1] - 1, 0)[None]], axis=0)


def x_down(v):
    return jnp.concatenate([pltpu.roll(v[3], 1, 0)[None], v[:3]], axis=0)


def first_plane(load, at):
    v = load(at)
    zp = pltpu.roll(v, v.shape[2] - 1, 2)
    zm = pltpu.roll(v, 1, 2)
    xp, xm = x_up(v), x_down(v)
    dz = zp - zm
    return v, dz, xp - xm, zp + zm, xp + xm, x_up(dz) - x_down(dz)


def edge(d, width, start, end):
    if d > 0:
        return slice(end - width, end), slice(start - width, start)
    if d < 0:
        return slice(start, start + width), slice(end, end + width)
    return slice(start, end), slice(start, end)


def walk(load, low, count, emit, straight=False):
    def step(at, carry):
        before, here = carry
        after = first_plane(load, at + 1)
        emit(
            at,
            here[0],
            here[4],
            before[0] + after[0],
            here[3],
            after[2] - before[2],
            here[5],
            after[1] - before[1],
        )
        return here[:3], after

    carry = (first_plane(load, low - 1)[:3], first_plane(load, low))
    if straight or count <= REACH:
        for k in range(count):
            carry = step(low + k, carry)
    else:
        lax.fori_loop(low, low + count, step, carry, unroll=count)


def dot_exact(values, table):
    hi = values.astype(jnp.bfloat16)
    rest = values - hi.astype(F32)
    mid = rest.astype(jnp.bfloat16)
    lo = (rest - mid.astype(F32)).astype(jnp.bfloat16)
    n = values.shape[0]
    out = jnp.dot(jnp.concatenate([hi, mid, lo], axis=0), table, preferred_element_type=F32)
    return out[:n] + out[n : 2 * n] + out[2 * n :]


def pick(values, lanes):
    return jnp.take_along_axis(values, lanes, axis=1, mode="promise_in_bounds")


def off_diagonal(coef, at, xs, ys, zs, dxy, dxz, dyz):
    return (
        (coef[0, at] * xs + coef[1, at] * ys + coef[2, at] * zs)
        + (coef[3, at] * dxy + coef[4, at] * dxz + coef[5, at] * dyz)
    )


def whole(ref):
    def load(at):
        return ref[at]

    return load


def relaxed(fields, at, v, *terms):
    coef, src, wgt = fields
    return (1.0 - DAMP) * v + wgt[at] * (src[at] - off_diagonal(coef, at, *terms))


def finish(one, coef, src, diag, wgt, up_out, res_out, two, up, res, sem):
    nx, ny, nz = up_out.shape
    cells = nx // 4

    def rows_of(out, y, value):
        flat = out.reshape(nx * ny, nz)
        for j in range(4):
            flat[pl.ds(j * ny + y, cells, stride=4 * ny), :] = value[j][1 : 1 + cells]

    def emit_two(at, v, *terms):
        value = relaxed((coef, src, wgt), at, v, *terms)
        two[at] = value
        if REACH <= at < REACH + ny:
            rows_of(up, at - REACH, value)

    walk(whole(one), REACH - 1, ny + 2, emit_two, straight=True)
    copies = [pltpu.make_async_copy(up, up_out, sem.at[0])]
    copies[0].start()

    def emit_last(at, v, *terms):
        rows_of(res, at - REACH, src[at] - (off_diagonal(coef, at, *terms) + diag[at] * v))

    half = ny // 2
    for n in range(2):
        rows = slice(n * half, (n + 1) * half)
        walk(whole(two), REACH + n * half, half, emit_last, straight=True)
        copies.append(pltpu.make_async_copy(res.at[:, rows], res_out.at[:, rows], sem.at[n + 1]))
        copies[-1].start()
    for copy in copies:
        copy.wait()


def kernel(
    gx_n, gy_n, p_in, d_in, c_in, one, coef, src, diag, wgt,
    pot, cor, den, two, fin,
    pool_c, pool_s, co, cs, wide, grown, corner,
    there, sent, got, local,
):
    nx, ny, nz = p_in.shape
    cols = nx // 4 + 2
    y0, y1, x0, x1 = REACH, REACH + ny, 4, 4 + nx
    gx = lax.axis_index("gx")
    gy = lax.axis_index("gy")

    def device(dx, dy):
        return (lax.rem(gx + dx + gx_n, gx_n), lax.rem(gy + dy + gy_n, gy_n))

    barrier = pltpu.get_barrier_semaphore()
    for i in [1, 6, 3, 4]:
        pl.semaphore_signal(barrier, inc=1, device_id=device(*NEIGHBOURS[i]), device_id_type=MESH)
    fields = ((p_in, pot, 3), (d_in, den, 2), (c_in, cor, 3))
    for k, (a, b, _) in enumerate(fields):
        for y in range(ny):
            pltpu.make_async_copy(a.at[:, y], b.at[y0 + y, x0:x1], local.at[k]).start()
    pl.semaphore_wait(barrier, 4)
    for n, which in enumerate(([1, 6], [3, 4])):
        for i in which:
            pl.semaphore_signal(
                there.at[n], inc=1, device_id=device(*NEIGHBOURS[i]), device_id_type=MESH)

    def take(rows, sem):
        ref = coef.reshape(coef.shape[0] * coef.shape[1] * 4 * cols, nz).at[0:rows]
        pltpu.make_async_copy(ref, ref, sem).wait()

    def remote(a, b, send, recv, to):
        pltpu.make_async_remote_copy(
            src_ref=a, dst_ref=b, send_sem=send, recv_sem=recv, device_id=device(*to), device_id_type=MESH,
        ).start()

    def send_halo(which, ks=(0, 1, 2)):
        for k in ks:
            _, ref, width = fields[k]
            for i in which:
                dx, dy = NEIGHBOURS[i]
                part, into = zip(edge(dy, width, y0, y1), edge(dx, width, x0, x1))
                sem = got.at[k // 2 + (2 if dy else 0)]
                remote(ref.at[part], ref.at[into], sent.at[0], sem, (dx, dy))

    strips = [(k, ref, w, n) for n in (0, 1) for k, (_, ref, w) in enumerate(fields)]

    for k in range(3):
        take(nx * ny, local.at[k])
        send_halo([1, 6], (k,))

    @pl.when(gy == 0)
    def _():
        for k, ref, w, n in strips:
            x = x1 - w if n else x0
            remote(
                ref.at[y0 : y0 + w, x : x + w], corner.at[n, k, 0:w, 0:w], sent.at[0], got.at[7], (0, -1))

    send_halo([4])
    send_halo([3])
    odd = lax.rem(gy, 2)
    pl.semaphore_wait(there.at[1 - odd], 2)
    send_halo([2, 7])

    @pl.when(gy != 0)
    def _():
        send_halo([0, 5])

    pl.semaphore_wait(there.at[odd], 2)
    wide[:, :, 14:16, :] = jnp.zeros((8, 3, 2, nz), F32)
    rows_x = [2 * ny * w for _, _, w in fields]
    rows_y = [nx * w + 2 * w * w for _, _, w in fields]

    rows_at = lax.broadcasted_iota(jnp.int32, (4 * nz, nz), 0)
    cols_at = lax.broadcasted_iota(jnp.int32, (4 * nz, nz), 1)
    group = nz // 4
    mean_table = jnp.where(
        (rows_at // nz) * group + (rows_at % nz) // 4 == cols_at, 1.0 / 64.0, 0.0
    ).astype(jnp.bfloat16)

    lane = lax.broadcasted_iota(jnp.int32, (cols, nz), 1)

    def block_mean(parts):
        at = 4 * (lane % group)
        sums = [(pick(p, at) + pick(p, at + 1)) + (pick(p, at + 2) + pick(p, at + 3)) for p in parts]
        low, high = jnp.where(lane < group, sums[0], sums[1]), jnp.where(lane < 3 * group, sums[2], sums[3])
        return (1.0 / 64.0) * jnp.where(lane < 2 * group, low, high)

    def by_rows(ref):
        def load(at):
            return jnp.stack([ref[at, pl.ds(j, cols, stride=4), :] for j in range(4)])

        return load

    def corrected(at):
        return fin[at] + grown[lax.div(at + 1, 4)][None]

    def build(at, v, xs, ys, zs, dxy, dxz, dyz):
        twice = 2.0 * v
        xx, yy, zz = 1.0 + (xs - twice), 1.0 + (ys - twice), 1.0 + (zs - twice)
        xy, xz, yz = 0.25 * dxy, 0.25 * dxz, 0.25 * dyz
        cxx = yy * zz - yz * yz
        cyy = xx * zz - xz * xz
        czz = xx * yy - xy * xy
        cxy = xz * yz - xy * zz
        cxz = xy * yz - xz * yy
        cyz = xy * xz - xx * yz
        src[at] = by_rows(den)(at) - (xx * cxx + xy * cxy + xz * cxz)
        main = -2.0 * (cxx + cyy + czz) - SCREEN
        diag[at], wgt[at] = main, DAMP / main
        coef[0, at], coef[1, at], coef[2, at] = cxx, cyy, czz
        coef[3, at], coef[4, at], coef[5, at] = 0.5 * cxy, 0.5 * cxz, 0.5 * cyz

    def sweep(load, into, low, count):
        def emit(at, v, *terms):
            into[at] = relaxed((coef, src, wgt), at, v, *terms)

        walk(load, low, count, emit)

    def residual_at(at, v, *terms):
        return src[at] - (off_diagonal(coef, at, *terms) + diag[at] * v)

    def emit_first(at, v, *terms):
        r = residual_at(at, v, *terms)
        pool_s[at - y0] = (r[0] + r[1]) + (r[2] + r[3])

    def pool_coef(block, planes, more):
        for f in range(6):
            total = pool_c[block, f] if more else None
            for y in planes:
                c = coef[f, y0 + 4 * block + y]
                c = (c[0] + c[1]) + (c[2] + c[3])
                total = c if total is None else total + c
            pool_c[block, f] = total

    def coarse_rows(dx, reach):
        if dx > 0:
            return slice(7 - reach, 7), slice(4 - reach, 4)
        if dx < 0:
            return slice(1, 1 + reach), slice(10, 10 + reach)
        return slice(1, 7), slice(4, 10)

    last = gy == gy_n - 1

    @pl.when(last)
    def _():
        take(2 * sum(w * w for _, _, w in fields), got.at[7])
        for k, ref, w, n in strips:
            x = x0 - w if n else x1
            remote(
                corner.at[n, k, 0:w, 0:w], ref.at[y1 : y1 + w, x : x + w],
                sent.at[1], got.at[2 + k // 2], (1 if n else -1, 0))

    take(rows_x[0] + rows_x[1], got.at[0])
    walk(by_rows(pot), y0 + 1, ny - 2, build)
    take(rows_x[2], got.at[1])
    sweep(by_rows(cor), one, y0 + 1, ny - 2)
    sweep(whole(one), two, y0 + 2, ny - 4)
    walk(whole(two), y0 + 3, ny - 6, emit_first)
    for block, planes in enumerate(((1, 2, 3), range(4), range(4), (0, 1, 2))):
        pool_coef(block, planes, False)

    take(2 * (rows_y[0] + rows_y[1]), got.at[2])
    for high in (0, 1):
        walk(by_rows(pot), y0 - 2 + high * (ny + 1), 3, build)
    pool_coef(0, (0,), True)
    pool_coef(3, (3,), True)
    parts = [pool_c[block].reshape(6 * cols, nz) for block in range(4)]
    means = dot_exact(jnp.concatenate(parts, axis=1), mean_table).reshape(6, cols, nz)
    co[0:6] = means
    far_first = (0, 2, 5, 7, 1, 6, 3, 4)
    for i in far_first:
        dx, dy = NEIGHBOURS[i]
        a, b = coarse_rows(dx, 4)
        remote(co.at[0:6, a], wide.at[0:6, 1 - dy, b], sent.at[0], got.at[4], (dx, dy))

    take(2 * rows_y[2], got.at[3])
    for high in (0, 1):
        sweep(by_rows(cor), one, y0 - 2 + high * (ny + 1), 3)
    for high in (0, 1):
        sweep(whole(one), two, y0 - 1 + high * (ny - 1), 3)
    for high in (0, 1):
        walk(whole(two), y0 + high * (ny - 3), 3, emit_first)
    parts = [
        (pool_s[4 * b] + pool_s[4 * b + 1]) + (pool_s[4 * b + 2] + pool_s[4 * b + 3]) for b in range(4)
    ]
    cs[...] = block_mean(parts)
    for i in far_first:
        dx, dy = NEIGHBOURS[i]
        a, b = coarse_rows(dx, 4)
        remote(cs.at[a], wide.at[6, 1 - dy, b], sent.at[0], got.at[5], (dx, dy))
    for i in far_first:
        dx, dy = NEIGHBOURS[i]
        if dx == 0:
            ys, yd = (slice(y1 - 3, y1 - 1), slice(0, 2)) if dy > 0 else (slice(y0 + 1, y0 + 3), slice(y1 + 1, y1 + 3))
            a, b = two.at[ys, :, 1 : cols - 1], fin.at[yd, :, 1 : cols - 1]
        else:
            ys, yd = edge(dy, 3, y0, y1)
            js = slice(1, 3) if dy == 0 else slice(1, 4) if dx > 0 else slice(0, 3)
            s, t = (cols - 2, 0) if dx > 0 else (1, cols - 1)
            a, b = two.at[ys, js, s], fin.at[yd, js, t]
        remote(a, b, sent.at[0], got.at[6], (dx, dy))
    rows_c = 6 * 6 * 4 + 2 * 6 * 6
    rows_s = 6 * 4 + 2 * 6
    rows_f = 2 * 2 * ny + 2 * 2 * nx + 4 * 9

    def keep(at, _):
        v = two[at]
        fin[at, 0, 1:cols, :] = v[0, 1:cols]
        fin[at, 1:3, 1 : cols - 1, :] = v[1:3, 1 : cols - 1]
        fin[at, 3, 0 : cols - 1, :] = v[3, 0 : cols - 1]
        return 0

    lax.fori_loop(y0, y1, keep, 0, unroll=8)
    for at in (y0 - 1, y1):
        fin[at, :, 1 : cols - 1, :] = two[at][:, 1 : cols - 1]
    wide[0:6, 1, 4:10, :] = co[0:6][:, 1:7]
    wide[6, 1, 4:10, :] = cs[...][1:7]

    take(rows_c, got.at[4])
    cc = [wide[f] for f in range(6)]
    spacing = 1.0 / 16.0
    coarse_w = DAMP / (-2.0 * spacing * (cc[0] + cc[1] + cc[2]) - SCREEN)
    cc = [spacing * c for c in cc]
    take(rows_s, got.at[5])
    coarse_b = wide[6]
    lane_3 = lax.broadcasted_iota(jnp.int32, (3, 16, nz), 2)
    in_group = lane_3 % group

    z_end, z_start = in_group == group - 1, in_group == 0

    def y_up(r):
        return jnp.where(lane_3 < nz - group, r, jnp.concatenate([r[1:], r[:1]], axis=0))

    def y_down(r):
        return jnp.where(lane_3 >= group, r, jnp.concatenate([r[2:], r[:2]], axis=0))

    value = coarse_w * coarse_b
    for _ in range(3):
        at = {
            k: pltpu.roll(value, -k % nz, 2)
            for h in (1, group - 1, group, group + 1, 2 * group - 1) for k in (h, -h)
        }
        zp = jnp.where(z_end, at[1 - group], at[1])
        zm = jnp.where(z_start, at[group - 1], at[-1])
        dz = zp - zm
        yp, ym = y_up(at[group]), y_down(at[-group])
        dy_ = yp - ym
        above = jnp.where(z_end, at[1], at[group + 1]) - jnp.where(z_start, at[2 * group - 1], at[group - 1])
        below = jnp.where(z_end, at[1 - 2 * group], at[1 - group]) - jnp.where(z_start, at[-1], at[-group - 1])
        xs = pltpu.roll(value, 15, 1) + pltpu.roll(value, 1, 1)
        dxy = pltpu.roll(dy_, 15, 1) - pltpu.roll(dy_, 1, 1)
        dxz = pltpu.roll(dz, 15, 1) - pltpu.roll(dz, 1, 1)
        dyz = y_up(above) - y_down(below)
        total = cc[0] * xs + cc[1] * (yp + ym) + cc[2] * (zp + zm)
        total = total + (cc[3] * dxy + cc[4] * dxz + cc[5] * dyz)
        value = (1.0 - DAMP) * value + coarse_w * (coarse_b - total)

    value = pltpu.roll(value, 13, 1)[:, 0:cols]
    for j, (blk, g) in enumerate(((0, 3), (1, 0), (1, 1), (1, 2), (1, 3), (2, 0))):
        grown[j] = pick(value[blk], g * group + lane // 4)

    take(rows_f, got.at[6])
    sweep(corrected, one, y0 - 2, ny + 4)
    take(sum(rows_x) + 2 * sum(rows_y) + rows_c + rows_s + rows_f, sent.at[0])

    @pl.when(last)
    def _():
        take(2 * sum(w * w for _, _, w in fields), sent.at[1])


def solution(mesh):
    gx_n, gy_n = mesh.shape["gx"], mesh.shape["gy"]

    def shards(potential, density, correction):
        nx, ny, nz = potential.shape
        cols = nx // 4 + 2
        rows = pltpu.VMEM((ny + 2 * REACH, 4 * cols, nz), F32)
        fine = pltpu.VMEM((ny + 2 * REACH, 4, cols, nz), F32)
        dma = pltpu.SemaphoreType.DMA
        field = (ny + 2 * REACH, 4, cols, nz)
        shape = jax.ShapeDtypeStruct(potential.shape, F32)
        fields = [jax.ShapeDtypeStruct(s, F32) for s in (field, (6, *field), field, field, field)]
        vmem, hbm = pl.BlockSpec(memory_space=pltpu.VMEM), pl.BlockSpec(memory_space=pltpu.HBM)
        parts = pl.pallas_call(
            functools.partial(kernel, gx_n, gy_n),
            out_shape=tuple(fields),
            in_specs=[pl.BlockSpec(memory_space=pl.ANY)] * 3,
            out_specs=[vmem] * 5,
            scratch_shapes=[
                rows, rows, rows, fine, fine,
                pltpu.VMEM((4, 6, cols, nz), F32), pltpu.VMEM((ny, cols, nz), F32),
                pltpu.VMEM((7, cols, nz), F32), pltpu.VMEM((cols, nz), F32),
                pltpu.VMEM((8, 3, 16, nz), F32), pltpu.VMEM((6, cols, nz), F32), pltpu.VMEM((2, 3, REACH, REACH, nz), F32),
                pltpu.SemaphoreType.REGULAR((2,)), dma((2,)), dma((8,)), dma((3,)),
            ],
            compiler_params=pltpu.CompilerParams(
                collective_id=0, has_side_effects=True, vmem_limit_bytes=30 * 1024 * 1024
            ),
        )(*[
            pltpu.with_memory_space_constraint(v, pltpu.HBM) for v in (potential, density, correction)
        ])
        return pl.pallas_call(
            finish,
            out_shape=(shape, shape),
            in_specs=[vmem] * 5,
            out_specs=[hbm] * 2,
            scratch_shapes=[fine, pltpu.VMEM(potential.shape, F32), pltpu.VMEM(potential.shape, F32), dma((3,))],
            compiler_params=pltpu.CompilerParams(vmem_limit_bytes=20 * 1024 * 1024),
        )(*parts)

    placed = (P("gx", "gy", None),) * 3
    return jax.shard_map(
        shards, mesh=mesh, in_specs=placed,
        out_specs=(P("gx", "gy", None), P("gx", "gy", None)), check_vma=False,
    )
```
